32 devices in a mesh: dp: 16 (over z, x, core), tensor: 2 (over y).
Axes of the slice: x: 2, y: 2, z: 4, core: 2. Of those that a mesh axis runs over, the one named last changes fastest.
Arguments:
- tokens: bfloat16 [12288, 1536], P('dp'), may hold values from -6 to 6
- lengths: int32 [48], P('dp'), may hold values from 1 to 256, 7680 in all
- qkv_weight: bfloat16 [1536, 2, 1024], P('dp', 'tensor'), may hold values from -0.15625 to 0.15625
- qkv_bias: bfloat16 [2, 1024], P('tensor'), may hold values from -3 to 3
- out_weight: bfloat16 [2, 768, 1536], P('tensor', None, 'dp'), may hold values from -0.875 to 0.875
- gate_weight: bfloat16 [1536, 8960], P('dp', 'tensor'), may hold values from -0.15625 to 0.15625
- up_weight: bfloat16 [1536, 8960], P('dp', 'tensor'), may hold values from -0.15625 to 0.15625
- down_weight: bfloat16 [8960, 1536], P('tensor', 'dp'), may hold values from -0.125 to 0.125
- attn_gain: bfloat16 [1536], replicated, may hold values from 0.5 to 1.5
- mlp_gain: bfloat16 [1536], replicated, may hold values from 0.5 to 1.5
- cotangent: bfloat16 [12288, 1536], P('dp'), may hold values from -6 to 6
Outputs:
- result: bfloat16 [12288, 1536], P('dp')
- grad_tokens: float32 [12288, 1536], P('dp')
- grad_qkv_weight: float32 [1536, 2, 1024], P('dp', 'tensor')
- grad_qkv_bias: float32 [2, 1024], P('tensor', 'dp')
- grad_out_weight: float32 [2, 768, 1536], P('tensor', None, 'dp')
- grad_gate_weight: float32 [1536, 8960], P('dp', 'tensor')
- grad_up_weight: float32 [1536, 8960], P('dp', 'tensor')
- grad_down_weight: float32 [8960, 1536], P('tensor', 'dp')
- grad_attn_gain: float32 [1536], P('dp')
- grad_mlp_gain: float32 [1536], P('dp')
The draws below stay inside these ranges and needn't reach their ends.
Inputs may be any that keep to these rules, and one draw needn't show every extreme that they name: Slots of sequence s from lengths[s] on are padding. All lengths add up to 7680, and the longest is 256.
All inputs are finite; a program needn't handle non-finite values. No bound on the sum of `lengths` on one device may be relied on, other than what follows from the above.
Results may differ from the reference program's by a relative error of at most 0.015.
Values may be sent and summed in bfloat16 or wider, within the bound.
No kernel may reach another device: no remote copies, remote signals or barrier semaphores. Data moves between devices by JAX's collectives and lax.ppermute only.
A program may use at most 256 MiB of HBM per device.

```python
import math
import jax
import jax.numpy as jnp
import numpy as np
from jax import lax

D = 1536
KV = 2
HD = 128
FF = 8960
SEQ = 256
G = 6
GC = 1024
SEQS = 48
TOKENS = 12288


def level_of(key, shape, cuts, smallest, top_value):
    loudness = 1.0
    for dim, shards_of in cuts:
        draws = jax.random.uniform(jax.random.fold_in(jax.random.fold_in(key, 6), dim), (shards_of,), jnp.float32, smallest / len(cuts), top_value / len(cuts))
        loudness = loudness * jnp.repeat(jnp.exp(draws), shape[dim] // shards_of).reshape((-1,) + (1,) * (len(shape) - 1 - dim))
    return loudness


def split_up(number_of, total, reach, slope):
    portions = [(1 << 20) // math.isqrt(grade ** slope) + 1 for grade in range(2, number_of + 1)]
    rest, given = total - reach - (number_of - 1), [1] * (number_of - 1)
    while rest > 0:
        candidates = [i for i in range(number_of - 1) if given[i] < reach]
        pool, left = sum([portions[i] for i in candidates]), rest
        for i in candidates:
            addition = min(reach - given[i], max(1, left * portions[i] // pool), rest)
            given[i] = given[i] + addition
            rest = rest - addition
    return np.array([reach] + given)


def ragged_sizes(rng, number_of, total, most, lean):
    if number_of == 2:
        one = jax.random.randint(rng, (), max(1, total - most), min(most, total - 1) + 1)
        return jnp.stack([one, total - one])
    sizes = jnp.asarray(split_up(number_of, total, most, lean), jnp.int32)
    twos = (number_of - 1) // 2
    giver, receiver = sizes[1:1 + 2 * twos:2], sizes[2:2 + 2 * twos:2]
    room = jnp.minimum(giver - 1, most - receiver)
    shifted = jax.random.randint(jax.random.fold_in(rng, 1), (twos,), 0, 1 << 20) % (room + 1)
    sizes = sizes.at[1:1 + 2 * twos:2].set(giver - shifted).at[2:2 + 2 * twos:2].set(receiver + shifted)
    return sizes[jax.random.permutation(jax.random.fold_in(rng, 2), number_of)]


def normal_values(key, extent, deviation, bound, split=(), held_as=jnp.bfloat16):
    factor_of = level_of(key, extent, split, -0.22, 0.18) if split else 1.0
    result = jax.random.normal(key, extent, jnp.float32) * deviation * factor_of
    return jnp.minimum(jnp.maximum(result, -bound), bound).astype(held_as)


def setup_inputs(seed: int = 0) -> dict:
    arg_keys = jax.random.split(jax.random.key(seed), 12)
    return {
        "tokens": normal_values(arg_keys[0], (TOKENS, D), 1.0, 6.0, ((0, 16),)),
        "lengths": ragged_sizes(arg_keys[1], SEQS, SEQS * SEQ * 5 // 8, SEQ, 2).astype(jnp.int32),
        "qkv_weight": normal_values(arg_keys[2], (D, KV, GC), D ** -0.5, 0.15625, ((0, 16), (1, 2))),
        "qkv_bias": normal_values(arg_keys[3], (KV, GC), 0.5, 3.0, ((0, 2),)),
        "out_weight": normal_values(arg_keys[4], (KV, G * HD, D), (KV * G * HD // 32) ** -0.5, 0.875, ((0, 2), (2, 16))),
        "gate_weight": normal_values(arg_keys[5], (D, FF), D ** -0.5, 0.15625, ((0, 16), (1, 2))),
        "up_weight": normal_values(arg_keys[6], (D, FF), D ** -0.5, 0.15625, ((0, 16), (1, 2))),
        "down_weight": normal_values(arg_keys[7], (FF, D), (FF // 4) ** -0.5, 0.125, ((0, 2), (1, 16))),
        "attn_gain": jnp.clip(1.0 + 0.1 * jax.random.normal(arg_keys[8], (D,), jnp.float32), 0.5, 1.5).astype(jnp.bfloat16),
        "mlp_gain": jnp.clip(1.0 + 0.1 * jax.random.normal(arg_keys[9], (D,), jnp.float32), 0.5, 1.5).astype(jnp.bfloat16),
        "cotangent": normal_values(arg_keys[10], (TOKENS, D), 1.0, 6.0, ((0, 16),)),
    }


epsilon = 1e-06
highest = lax.Precision.HIGHEST

@jax.custom_vjp
def low(v):
    return lax.optimization_barrier(v.astype(jnp.bfloat16)).astype(jnp.float32)

@jax.custom_vjp
def low_back(v):
    return v

def low_keep(v):
    return (low(v), None)

def low_pass(kept, grad):
    return (grad,)

def back_keep(v):
    return (v, None)

def back_low(kept, grad):
    return (low(grad),)
low.defvjp(low_keep, low_pass)
low_back.defvjp(back_keep, back_low)

def normalize(values):
    inverse = lax.rsqrt(lax.optimization_barrier(jnp.mean(values * values, axis=-1, keepdims=True)) + epsilon)
    return values * inverse

def rotary_tables(length, head_size):
    half_size = head_size // 2
    frequency = jnp.power(10000.0, -jnp.arange(half_size, dtype=jnp.float32) * 2.0 / head_size)
    angles = jnp.arange(length, dtype=jnp.float32)[:, None] * frequency[None, :]
    angles = jnp.concatenate([angles, angles], axis=-1)
    return (jnp.cos(angles), jnp.sin(angles))

def rotate(values, cosine_table, sine_table):
    half_size = values.shape[-1] // 2
    turned = jnp.concatenate([-values[..., half_size:], values[..., :half_size]], axis=-1)
    return values * cosine_table + turned * sine_table

def attend(pieces):
    queries, key_rows, value_rows, length = pieces
    scores = jnp.einsum('qhgd,khd->hgqk', queries, key_rows, precision=highest) * HD ** (-0.5)
    scores = low_back(scores)
    positions = jnp.arange(SEQ)
    visible = (positions[None, :] <= positions[:, None]) & (positions[None, :] < length)
    scores = jnp.where(visible, scores, -jnp.inf)
    weights = jax.nn.softmax(scores, axis=-1)
    return jnp.einsum('hgqk,khd->qhgd', low(weights), value_rows, precision=highest)

def layer_forward(inputs, qkv_weight, qkv_bias, out_weight, gate_weight, up_weight, down_weight, attn_gain, mlp_gain, lengths):
    normed = low(normalize(inputs) * attn_gain)
    mixed = jnp.einsum('td,dhc->thc', normed, qkv_weight, precision=highest) + qkv_bias
    mixed = low_back(mixed)
    query_cols = G * HD
    cosine_table, sine_table = rotary_tables(SEQ, HD)
    queries = mixed[:, :, :query_cols].reshape(SEQS, SEQ, KV, G, HD)
    queries = low(rotate(queries, cosine_table[None, :, None, None, :], sine_table[None, :, None, None, :]))
    key_rows = mixed[:, :, query_cols:query_cols + HD].reshape(SEQS, SEQ, KV, HD)
    key_rows = low(rotate(key_rows, cosine_table[None, :, None, :], sine_table[None, :, None, :]))
    value_rows = low(mixed[:, :, query_cols + HD:]).reshape(SEQS, SEQ, KV, HD)
    context = lax.map(jax.checkpoint(attend), (queries, key_rows, value_rows, lengths))
    context = low(low_back(context.reshape(TOKENS, KV, query_cols)))
    branch = low_back(jnp.einsum('thc,hcd->td', context, out_weight, precision=highest))
    hidden_state = inputs + branch
    second = low(normalize(hidden_state) * mlp_gain)
    gate_value = low_back(jnp.dot(second, gate_weight, precision=highest))
    up_value = low_back(jnp.dot(second, up_weight, precision=highest))
    activation = low(jax.nn.silu(gate_value) * up_value)
    return hidden_state + low_back(jnp.dot(activation, down_weight, precision=highest))

def reference(tokens, lengths, qkv_weight, qkv_bias, out_weight, gate_weight, up_weight, down_weight, attn_gain, mlp_gain, cotangent):
    floats = (tokens.astype(jnp.float32), qkv_weight.astype(jnp.float32), qkv_bias.astype(jnp.float32), out_weight.astype(jnp.float32), gate_weight.astype(jnp.float32), up_weight.astype(jnp.float32), down_weight.astype(jnp.float32), attn_gain.astype(jnp.float32), mlp_gain.astype(jnp.float32))

    def forward(inputs, qkv_w, qkv_b, out_w, gate_w, up_w, down_w, gain_one, gain_two):
        return layer_forward(inputs, qkv_w, qkv_b, out_w, gate_w, up_w, down_w, gain_one, gain_two, lengths)
    output, pullback = jax.vjp(forward, *floats)
    valid_rows = (jnp.arange(SEQ)[None, :] < lengths[:, None]).reshape(TOKENS).astype(jnp.float32)
    seed_grad = cotangent.astype(jnp.float32) * valid_rows[:, None]
    grads_all = pullback(seed_grad)
    return (output.astype(jnp.bfloat16), grads_all[0], grads_all[1], grads_all[2], grads_all[3], grads_all[4], grads_all[5], grads_all[6], grads_all[7], grads_all[8])
```

```python
import jax
import jax.numpy as jnp
from jax import lax
from jax.sharding import Mesh
from jax.sharding import PartitionSpec as P

epsilon = 1e-06
SWAP = [(0, 1), (1, 0)]
bf16 = jnp.bfloat16
f32 = jnp.float32


def inverse_rms(values):
    return lax.rsqrt(jnp.mean(values * values, axis=-1, keepdims=True) + epsilon)


def norm_backward(grad_normed, normed_rows, inverse):
    return inverse * (
        grad_normed - normed_rows * jnp.mean(grad_normed * normed_rows, axis=-1, keepdims=True)
    )


def rotary_tables(length, head_size):
    half_size = head_size // 2
    frequency = jnp.power(10000.0, -jnp.arange(half_size, dtype=f32) * 2.0 / head_size)
    angles = jnp.arange(length, dtype=f32)[:, None] * frequency[None, :]
    angles = jnp.concatenate([angles, angles], axis=-1)
    return (jnp.cos(angles), jnp.sin(angles))


def rotate(values, cosine_table, sine_table):
    half_size = values.shape[-1] // 2
    turned = jnp.concatenate([-values[..., half_size:], values[..., :half_size]], axis=-1)
    return values * cosine_table + turned * sine_table


def rotate_back(gradient, cosine_table, sine_table):
    half_size = gradient.shape[-1] // 2
    scaled = gradient * sine_table
    turned = jnp.concatenate([scaled[..., half_size:], -scaled[..., :half_size]], axis=-1)
    return gradient * cosine_table + turned


def swap(value, axis):
    return lax.ppermute(value, axis, SWAP)


def gather_rows(shard):
    own = lax.all_gather(shard, "o", axis=0, tiled=True)
    beside = swap(own, "m")
    return jnp.concatenate([own, beside, swap(own, "c"), swap(beside, "c")], axis=0)


def scatter_rows(near, far):
    half = near.shape[0] // 2
    both = near + swap(far.astype(bf16), "c").astype(f32)
    mine = both[:half] + swap(both[half:].astype(bf16), "m").astype(f32)
    return lax.psum_scatter(mine.astype(bf16), "o", scatter_dimension=0, tiled=True).astype(f32)


def tensor_sum(part):
    low = lax.optimization_barrier(part.astype(bf16))
    return low.astype(f32) + swap(low, "tensor").astype(f32)


def weight_grad(rows, columns):
    half = rows.shape[1] // 2
    far = jnp.einsum("td,tn->dn", rows[:, half:], columns, preferred_element_type=f32)
    near = jnp.einsum("td,tn->dn", rows[:, :half], columns, preferred_element_type=f32)
    return near, far


def local(
    tokens,
    lengths,
    qkv_weight,
    qkv_bias,
    out_weight,
    gate_weight,
    up_weight,
    down_weight,
    attn_gain,
    mlp_gain,
    cotangent,
):
    token_rows, width = tokens.shape
    seqs_here = lengths.shape[0]
    seq_len = token_rows // seqs_here
    group_cols = out_weight.shape[1]
    mixed_cols = qkv_weight.shape[2]
    head_size = (mixed_cols - group_cols) // 2
    groups = group_cols // head_size
    score_scale = head_size ** (-0.5)
    shard_rows = qkv_weight.shape[0]
    outer = width // shard_rows // 4
    my_m, my_c = lax.axis_index("m"), lax.axis_index("c")

    attn_shard = jnp.concatenate([qkv_weight[:, 0, :], out_weight[0].T], axis=1)
    attn_full = gather_rows(attn_shard)
    gate_full = gather_rows(gate_weight)
    up_full = gather_rows(up_weight)
    down_full = gather_rows(down_weight.T)
    qkv_full, out_full = attn_full[:, :mixed_cols], attn_full[:, mixed_cols:]

    j = jnp.arange(width)
    block, row = j // shard_rows, j % shard_rows
    far_c, far_m, at_o = block // (2 * outer), block // outer % 2, block % outer
    place = ((at_o * 2 + (far_m ^ my_m)) * 2 + (far_c ^ my_c)) * shard_rows + row
    order = (jnp.arange(width)[:, None] == place[None, :]).astype(bf16)
    token_low = jnp.dot(tokens, order, preferred_element_type=bf16)
    seed_all = jnp.dot(cotangent, order, preferred_element_type=bf16)
    gains = jnp.dot(jnp.stack([attn_gain, mlp_gain]), order, preferred_element_type=f32)
    attn_gain_f, mlp_gain_f = gains[0], gains[1]

    token_float = token_low.astype(f32)
    first_inverse = inverse_rms(token_float)
    first_rows = token_float * first_inverse
    first_normed = (first_rows * attn_gain_f).astype(bf16)
    mixed_rows = jnp.dot(first_normed, qkv_full, preferred_element_type=f32)
    mixed_rows = mixed_rows + qkv_bias.astype(f32)
    cosine_table, sine_table = rotary_tables(seq_len, head_size)
    cosine_query = cosine_table[None, :, None, :]
    sine_query = sine_table[None, :, None, :]
    query_raw = mixed_rows[:, :group_cols].reshape(seqs_here, seq_len, groups, head_size)
    key_raw = mixed_rows[:, group_cols : group_cols + head_size].reshape(
        seqs_here, seq_len, head_size
    )
    value_low = (
        mixed_rows[:, group_cols + head_size :].astype(bf16).reshape(seqs_here, seq_len, head_size)
    )
    queries = rotate(query_raw, cosine_query, sine_query).astype(bf16)
    key_low = rotate(key_raw, cosine_table, sine_table).astype(bf16)
    positions = jnp.arange(seq_len)
    causal = (positions[None, :] <= positions[:, None])[None, None, :, :]
    inside = positions[None, None, None, :] < lengths[:, None, None, None]
    visible = causal & inside
    scores = (
        jnp.einsum("bqgd,bkd->bgqk", queries, key_low, preferred_element_type=f32) * score_scale
    )
    scores = jnp.where(visible, scores, -jnp.inf)
    score_peak = jnp.max(scores, axis=-1, keepdims=True)
    exp_total = jnp.sum(jnp.exp(scores - score_peak), axis=-1, keepdims=True)
    log_total = score_peak + jnp.log(exp_total)
    probs_low = jnp.exp(scores - log_total).astype(bf16)
    context = jnp.einsum("bgqk,bkd->bqgd", probs_low, value_low, preferred_element_type=f32)
    context_low = context.astype(bf16).reshape(token_rows, group_cols)
    attn_part = jnp.einsum("tc,dc->td", context_low, out_full, preferred_element_type=f32)
    attn_total = tensor_sum(attn_part)
    hidden_state = token_float + attn_total
    second_inverse = inverse_rms(hidden_state)
    second_rows = hidden_state * second_inverse
    second_normed = (second_rows * mlp_gain_f).astype(bf16)
    gate_value = jnp.dot(second_normed, gate_full, preferred_element_type=f32)
    up_value = jnp.dot(second_normed, up_full, preferred_element_type=f32)
    sigmoid_gate = jax.nn.sigmoid(gate_value)
    silu_gate = gate_value * sigmoid_gate
    activation = (silu_gate * up_value).astype(bf16)
    valid_rows = (positions[None, :] < lengths[:, None]).reshape(token_rows, 1)
    seed_low = jnp.where(valid_rows, seed_all, jnp.zeros_like(seed_all))
    seed_grad = seed_low.astype(f32)
    down_share = scatter_rows(*weight_grad(seed_low, activation))
    mlp_part = jnp.einsum("tf,df->td", activation, down_full, preferred_element_type=f32)
    mlp_total = tensor_sum(mlp_part)
    result = jnp.einsum(
        "tj,dj->td", (hidden_state + mlp_total).astype(bf16), order, preferred_element_type=bf16
    )
    grad_act = jnp.dot(seed_low, down_full, preferred_element_type=f32)
    grad_gate = (
        grad_act * up_value * sigmoid_gate * (1.0 + gate_value * (1.0 - sigmoid_gate))
    ).astype(bf16)
    grad_up = (grad_act * silu_gate).astype(bf16)
    gate_share = scatter_rows(*weight_grad(second_normed, grad_gate))
    up_share = scatter_rows(*weight_grad(second_normed, grad_up))
    second_part = jnp.einsum("tf,df->td", grad_gate, gate_full, preferred_element_type=f32)
    second_part = second_part + jnp.einsum(
        "tf,df->td", grad_up, up_full, preferred_element_type=f32
    )
    second_grad = tensor_sum(second_part)
    grad_mlp_gain = jnp.sum(second_grad * second_rows, axis=0)
    hidden_grad = seed_grad + norm_backward(second_grad * mlp_gain_f, second_rows, second_inverse)
    hidden_low = hidden_grad.astype(bf16)
    grad_context = jnp.dot(hidden_low, out_full, preferred_element_type=f32)
    grad_context = grad_context.astype(bf16).reshape(seqs_here, seq_len, groups, head_size)
    again_scores = (
        jnp.einsum("bqgd,bkd->bgqk", queries, key_low, preferred_element_type=f32) * score_scale
    )
    again_scores = jnp.where(visible, again_scores, -jnp.inf)
    probs = jnp.exp(again_scores - log_total)
    probs_again = probs.astype(bf16)
    grad_probs = jnp.einsum("bqgd,bkd->bgqk", grad_context, value_low, preferred_element_type=f32)
    grad_value = jnp.einsum(
        "bgqk,bqgd->bkd", probs_again, grad_context, preferred_element_type=f32
    )
    row_inner = jnp.sum(grad_probs * probs, axis=-1, keepdims=True)
    grad_scores = (probs * (grad_probs - row_inner)).astype(bf16)
    grad_query = (
        jnp.einsum("bgqk,bkd->bqgd", grad_scores, key_low, preferred_element_type=f32)
        * score_scale
    )
    grad_key = (
        jnp.einsum("bgqk,bqgd->bkd", grad_scores, queries, preferred_element_type=f32)
        * score_scale
    )
    grad_query = rotate_back(grad_query, cosine_query, sine_query)
    grad_key = rotate_back(grad_key, cosine_table, sine_table)
    grad_mixed = jnp.concatenate(
        [
            grad_query.reshape(token_rows, group_cols),
            grad_key.reshape(token_rows, head_size),
            grad_value.reshape(token_rows, head_size),
        ],
        axis=-1,
    ).astype(bf16)
    first_part = jnp.einsum("tc,dc->td", grad_mixed, qkv_full, preferred_element_type=f32)
    first_grad = tensor_sum(first_part)
    grad_attn_gain = jnp.sum(first_grad * first_rows, axis=0)
    input_grad = hidden_grad + norm_backward(first_grad * attn_gain_f, first_rows, first_inverse)
    high = lax.reduce_precision(input_grad, 8, 7)
    rest = (input_grad - high).astype(bf16)
    grad_tokens = jnp.einsum(
        "tj,dj->td", high.astype(bf16), order, preferred_element_type=f32
    ) + jnp.einsum("tj,dj->td", rest, order, preferred_element_type=f32)

    grad_bias = jnp.sum(grad_mixed.astype(f32), axis=0).reshape(outer, 2, 2, -1)
    bias_rows = grad_bias.shape[-1]
    grad_bias = jnp.where(my_c == 1, grad_bias[:, :, ::-1], grad_bias)
    grad_bias = jnp.where(my_m == 1, grad_bias[:, ::-1], grad_bias)
    grad_bias = jnp.pad(
        grad_bias.transpose(2, 1, 0, 3), ((0, 0), (0, 0), (0, 0), (0, shard_rows - bias_rows))
    ).reshape(width)
    vectors = jnp.stack([grad_attn_gain, grad_mlp_gain, grad_bias], axis=1)
    vectors = jnp.pad(vectors, ((0, 0), (0, 125)))
    near_qkv, far_qkv = weight_grad(first_normed, grad_mixed)
    near_out, far_out = weight_grad(hidden_low, context_low)
    half = width // 2
    attn_share = scatter_rows(
        jnp.concatenate([near_qkv, near_out, vectors[:half]], axis=1),
        jnp.concatenate([far_qkv, far_out, vectors[half:]], axis=1),
    )
    vector_share = attn_share[:, mixed_cols + group_cols :]
    return (
        result,
        grad_tokens,
        attn_share[:, None, :mixed_cols],
        vector_share[None, :bias_rows, 2],
        attn_share[:, mixed_cols : mixed_cols + group_cols].T[None],
        gate_share,
        up_share,
        down_share.T,
        vector_share[:, 0],
        vector_share[:, 1],
    )


def solution(mesh):
    dp, tensor = mesh.shape["dp"], mesh.shape["tensor"]
    fine = Mesh(mesh.devices.reshape(dp // 4, 2, 2, tensor), ("o", "m", "c", "tensor"))
    data = ("o", "m", "c")
    return jax.shard_map(
        local,
        mesh=fine,
        in_specs=(
            P(data, None),
            P(data),
            P(data, "tensor", None),
            P("tensor", None),
            P("tensor", None, data),
            P(data, "tensor"),
            P(data, "tensor"),
            P("tensor", data),
            P(),
            P(),
            P(data, None),
        ),
        out_specs=(
            P(data, None),
            P(data, None),
            P(data, "tensor", None),
            P("tensor", data),
            P("tensor", None, data),
            P(data, "tensor"),
            P(data, "tensor"),
            P("tensor", data),
            P(data),
            P(data),
        ),
        check_vma=False,
    )
```

```python
import jax
import jax.numpy as jnp
from jax import lax
from jax.experimental import pallas as pl
from jax.experimental.pallas import tpu as pltpu
from jax.sharding import Mesh
from jax.sharding import PartitionSpec as P


epsilon = 1e-06
SWAP = [(0, 1), (1, 0)]
bf16 = jnp.bfloat16
f32 = jnp.float32


def inverse_rms(values):
    return lax.rsqrt(jnp.mean(values * values, axis=-1, keepdims=True) + epsilon)


def norm_backward(grad_normed, normed_rows, inverse):
    return inverse * (
        grad_normed - normed_rows * jnp.mean(grad_normed * normed_rows, axis=-1, keepdims=True)
    )


def rotary_tables(length, head_size):
    half_size = head_size // 2
    frequency = jnp.power(10000.0, -jnp.arange(half_size, dtype=f32) * 2.0 / head_size)
    angles = jnp.arange(length, dtype=f32)[:, None] * frequency[None, :]
    angles = jnp.concatenate([angles, angles], axis=-1)
    return (jnp.cos(angles), jnp.sin(angles))


def swap(value, axis):
    return lax.ppermute(value, axis, SWAP)


def gather_rows(shard):
    own = lax.all_gather(shard, "o", axis=0, tiled=True)
    beside = swap(own, "m")
    return (own, beside, swap(own, "c"), swap(beside, "c"))


def scatter_z(rows):
    return lax.psum_scatter(rows.astype(bf16), "o", scatter_dimension=0, tiled=True)


def scatter_z_direct(rows):
    outer = lax.axis_size("o")
    me = lax.axis_index("o")
    blocks = rows.reshape(outer, rows.shape[0] // outer, rows.shape[1])
    total = lax.dynamic_index_in_dim(blocks, me, 0, False)
    low = blocks.astype(bf16)
    for shift in range(1, outer):
        block = lax.dynamic_index_in_dim(low, lax.rem(me + shift, outer), 0, False)
        ring = [(i, (i + shift) % outer) for i in range(outer)]
        total = total + lax.ppermute(block, "o", ring).astype(f32)
    return total


def scatter_grad(lefts, rights, extra=None, way="xz"):
    width = lefts[0].shape[1]
    half, quarter = width // 2, width // 4

    def rows(start, stop):
        pieces = [
            matmul("td,tn->dn", left[:, start:stop], right)
            for left, right in zip(lefts, rights)
        ]
        if extra is not None:
            pieces.append(extra[start:stop])
        return pieces[0] if len(pieces) == 1 else jnp.concatenate(pieces, axis=1)

    came = swap(rows(half, width).astype(bf16), "c")
    sent = rows(quarter, half) + came[quarter:].astype(f32)
    kept = rows(0, quarter) + came[:quarter].astype(f32)
    if way == "zx":
        beside = swap(scatter_z(sent), "m")
        return scatter_z(kept).astype(f32) + beside.astype(f32)
    kept = kept + swap(sent.astype(bf16), "m").astype(f32)
    return scatter_z_direct(kept) if way == "direct" else scatter_z(kept).astype(f32)


def tensor_sum(part):
    return part.astype(f32) + swap(part, "tensor").astype(f32)


def matmul(spec, left, right):
    return jnp.einsum(spec, left, right, preferred_element_type=f32)


def tile_of(columns):
    return 512 if columns % 512 == 0 else 640


def whole(shape):
    return pl.BlockSpec(shape, lambda i: (0, 0))


def column_tile(rows, tile):
    return pl.BlockSpec((rows, tile), lambda i: (0, i))


def run(kernel, grid, in_specs, out_specs, out_shape, args, flops, scratch=()):
    moved = sum(a.size * a.dtype.itemsize for a in (*args, *out_shape))
    return pl.pallas_call(
        kernel,
        grid=(grid,),
        in_specs=in_specs,
        out_specs=out_specs,
        out_shape=out_shape,
        scratch_shapes=scratch,
        compiler_params=pltpu.CompilerParams(
            dimension_semantics=("arbitrary",), vmem_limit_bytes=56 << 20
        ),
        cost_estimate=pl.CostEstimate(flops=flops, bytes_accessed=moved, transcendentals=0),
    )(*args)


def stacked(refs):
    return jnp.concatenate([ref[...] for ref in refs], axis=0)


def gate_up(normed, gate, up):
    tokens, width = normed.shape
    columns = gate[0].shape[1]
    tile = tile_of(columns)

    def kernel(a_ref, *refs):
        gate_out, up_out, act_out = refs[8:]
        a = a_ref[...]
        g = jnp.dot(a, stacked(refs[:4]), preferred_element_type=f32)
        u = jnp.dot(a, stacked(refs[4:8]), preferred_element_type=f32)
        gate_out[...] = g
        up_out[...] = u
        act_out[...] = (g * jax.nn.sigmoid(g) * u).astype(bf16)

    out = column_tile(tokens, tile)
    return run(
        kernel,
        columns // tile,
        [whole((tokens, width))] + [column_tile(width // 4, tile)] * 8,
        [out] * 3,
        [jax.ShapeDtypeStruct((tokens, columns), t) for t in (f32, f32, bf16)],
        (normed, *gate, *up),
        4 * tokens * width * columns,
    )


def gate_up_backward(seed, down, gate, up):
    tokens, width = seed.shape
    columns = gate.shape[1]
    tile = tile_of(columns)

    def kernel(a_ref, d0, d1, d2, d3, gate_ref, up_ref, grad_gate, grad_up):
        grad = jnp.dot(a_ref[...], stacked((d0, d1, d2, d3)), preferred_element_type=f32)
        g, u = gate_ref[...], up_ref[...]
        sigmoid = jax.nn.sigmoid(g)
        grad_gate[...] = (grad * u * sigmoid * (1.0 + g * (1.0 - sigmoid))).astype(bf16)
        grad_up[...] = (grad * (g * sigmoid)).astype(bf16)

    tiles = column_tile(tokens, tile)
    return run(
        kernel,
        columns // tile,
        [whole((tokens, width))] + [column_tile(width // 4, tile)] * 4 + [tiles] * 2,
        [tiles] * 2,
        [jax.ShapeDtypeStruct((tokens, columns), bf16)] * 2,
        (seed, *down, gate, up),
        2 * tokens * width * columns,
    )


def back_product(values, weights, before, out_type):
    tokens, columns = values[0].shape
    quarter = weights[0][0].shape[0]
    width = 4 * quarter
    tile = tile_of(columns)
    pairs = len(values)
    steps = columns // tile

    def kernel(*refs):
        value_refs, weight_refs = refs[:pairs], refs[pairs : 5 * pairs]
        out_ref, total = refs[-2:]
        step = pl.program_id(0)

        @pl.when(step == 0)
        def _():
            total[...] = jnp.zeros_like(total) if before is None else refs[5 * pairs][...]

        for piece in range(4):
            part = None
            for pair in range(pairs):
                term = lax.dot_general(
                    value_refs[pair][...],
                    weight_refs[4 * pair + piece][...],
                    (((1,), (1,)), ((), ())),
                    preferred_element_type=f32,
                )
                part = term if part is None else part + term
            total[:, piece * quarter : (piece + 1) * quarter] += part

        @pl.when(step == steps - 1)
        def _():
            out_ref[...] = total[...].astype(out_type)

    args = (*values, *(piece for weight in weights for piece in weight))
    specs = [column_tile(tokens, tile)] * pairs + [column_tile(quarter, tile)] * (4 * pairs)
    if before is not None:
        args, specs = args + (before,), specs + [whole((tokens, width))]
    return run(
        kernel,
        steps,
        specs,
        [whole((tokens, width))],
        [jax.ShapeDtypeStruct((tokens, width), out_type)],
        args,
        2 * pairs * tokens * width * columns,
        [pltpu.VMEM((tokens, width), f32)],
    )[0]


def dot_nt(left, right):
    return lax.dot_general(left, right, (((1,), (1,)), ((), ())), preferred_element_type=f32)


def dot_tn(left, right):
    return lax.dot_general(left, right, (((0,), (0,)), ((), ())), preferred_element_type=f32)


def visible_keys(length, size):
    query = lax.broadcasted_iota(jnp.int32, (size, size), 0)
    key = lax.broadcasted_iota(jnp.int32, (size, size), 1)
    return (key <= query) & (key < length)


def softmax_of(query, key, visible, scale):
    scores = jnp.where(visible, dot_nt(query, key) * scale, -jnp.inf)
    powers = jnp.exp(scores - jnp.max(scores, axis=-1, keepdims=True))
    return powers / jnp.sum(powers, axis=-1, keepdims=True)


def attention(normed, pieces, bias, cosine, sine, lengths, head):
    tokens, width = normed.shape
    seqs, size = lengths.shape[0], tokens // lengths.shape[0]
    quarter, mixed_cols = width // 4, bias.shape[1]
    group_cols = mixed_cols - 2 * head

    def kernel(len_ref, a_ref, p0, p1, p2, p3, bias_ref, cos_ref, sin_ref, low, context, out):
        weights = (p0, p1, p2, p3)
        weight = jnp.concatenate([ref[:, :mixed_cols] for ref in weights], axis=0)
        mixed = jnp.dot(a_ref[...], weight, preferred_element_type=f32) + bias_ref[...]
        cos, sin = cos_ref[...], sin_ref[...]

        def rope(value):
            return (value * cos + pltpu.roll(value, head // 2, 1) * sin).astype(bf16)

        key = rope(mixed[:, group_cols : group_cols + head])
        value = mixed[:, group_cols + head :].astype(bf16)
        low[:, group_cols : group_cols + head] = key
        low[:, group_cols + head :] = value
        visible = visible_keys(len_ref[pl.program_id(0)], size)
        for start in range(0, group_cols, head):
            query = rope(mixed[:, start : start + head])
            low[:, start : start + head] = query
            probs = softmax_of(query, key, visible, head**-0.5).astype(bf16)
            context[:, start : start + head] = jnp.dot(
                probs, value, preferred_element_type=f32
            ).astype(bf16)
        for piece in range(4):
            out[:, piece * quarter : (piece + 1) * quarter] = dot_nt(
                context[...], weights[piece][:, mixed_cols:]
            ).astype(bf16)

    def rows(columns):
        return pl.BlockSpec((size, columns), lambda i: (i, 0))

    return run(
        kernel,
        seqs,
        [pl.BlockSpec(memory_space=pltpu.SMEM), rows(width)]
        + [whole(pieces[0].shape)] * 4
        + [whole(bias.shape), whole(cosine.shape), whole(sine.shape)],
        [rows(mixed_cols), rows(group_cols), rows(width)],
        [jax.ShapeDtypeStruct((tokens, c), bf16) for c in (mixed_cols, group_cols, width)],
        (lengths, normed, *pieces, bias, cosine, sine),
        2 * tokens * width * (mixed_cols + group_cols),
    )


def attention_backward(hidden_low, low, pieces, cosine, sine, lengths, normal, head):
    tokens, width = hidden_low.shape
    seqs, size = lengths.shape[0], tokens // lengths.shape[0]
    quarter, mixed_cols = width // 4, low.shape[1]
    group_cols = mixed_cols - 2 * head
    scale = head**-0.5

    def kernel(
        len_ref, h_ref, low_ref, p0, p1, p2, p3, cos_ref, sin_ref, normal_ref, mixed, part, bias, gain
    ):
        weights = (p0, p1, p2, p3)
        cos, sin = cos_ref[...], sin_ref[...]

        @pl.when(pl.program_id(0) == 0)
        def _():
            bias[...] = jnp.zeros_like(bias)
            gain[...] = jnp.zeros_like(gain)

        def keep(start, value, turn):
            if turn:
                value = value * cos - pltpu.roll(value, head // 2, 1) * sin
            rounded = value.astype(bf16)
            mixed[:, start : start + head] = rounded
            bias[:, start : start + head] += jnp.sum(
                rounded.astype(f32), axis=0, keepdims=True
            )

        out_weight = jnp.concatenate([ref[:, mixed_cols:] for ref in weights], axis=0)
        grad_context = jnp.dot(h_ref[...], out_weight, preferred_element_type=f32).astype(bf16)
        key = low_ref[:, group_cols : group_cols + head]
        value = low_ref[:, group_cols + head :]
        visible = visible_keys(len_ref[pl.program_id(0)], size)
        grad_key = jnp.zeros((size, head), f32)
        grad_value = jnp.zeros((size, head), f32)
        for start in range(0, group_cols, head):
            query = low_ref[:, start : start + head]
            grad = grad_context[:, start : start + head]
            probs = softmax_of(query, key, visible, scale)
            grad_value += dot_tn(probs.astype(bf16), grad)
            grad_probs = dot_nt(grad, value)
            inner = jnp.sum(grad_probs * probs, axis=-1, keepdims=True)
            grad_scores = (probs * (grad_probs - inner)).astype(bf16)
            grad_key += dot_tn(grad_scores, query)
            keep(start, jnp.dot(grad_scores, key, preferred_element_type=f32) * scale, True)
        keep(group_cols, grad_key * scale, True)
        keep(group_cols + head, grad_value, False)
        for piece in range(4):
            columns = slice(piece * quarter, (piece + 1) * quarter)
            term = dot_nt(mixed[...], weights[piece][:, :mixed_cols])
            part[:, columns] = term.astype(bf16)
            gain[:, columns] += jnp.sum(term * normal_ref[:, columns], axis=0, keepdims=True)

    def rows(columns):
        return pl.BlockSpec((size, columns), lambda i: (i, 0))

    return run(
        kernel,
        seqs,
        [pl.BlockSpec(memory_space=pltpu.SMEM), rows(width), rows(mixed_cols)]
        + [whole(pieces[0].shape)] * 4
        + [whole(cosine.shape), whole(sine.shape), rows(width)],
        [rows(mixed_cols), rows(width), whole((1, mixed_cols)), whole((1, width))],
        [
            jax.ShapeDtypeStruct((tokens, mixed_cols), bf16),
            jax.ShapeDtypeStruct((tokens, width), bf16),
            jax.ShapeDtypeStruct((1, mixed_cols), f32),
            jax.ShapeDtypeStruct((1, width), f32),
        ],
        (lengths, hidden_low, low, *pieces, cosine, sine, normal),
        2 * tokens * width * (mixed_cols + group_cols),
    )


def layer(
    tokens,
    lengths,
    qkv_weight,
    qkv_bias,
    out_weight,
    gate_weight,
    up_weight,
    down_weight,
    attn_gain,
    mlp_gain,
    cotangent,
):
    token_rows, width = tokens.shape
    seqs_here = lengths.shape[0]
    seq_len = token_rows // seqs_here
    group_cols = out_weight.shape[1]
    mixed_cols = qkv_weight.shape[2]
    head_size = (mixed_cols - group_cols) // 2
    shard_rows = qkv_weight.shape[0]
    outer = width // shard_rows // 4
    my_m, my_c = lax.axis_index("m"), lax.axis_index("c")

    attn_shard = jnp.concatenate([qkv_weight[:, 0, :], out_weight[0].T], axis=1)
    attn_pieces = gather_rows(attn_shard)
    hidden = gate_weight.shape[1]
    cut = hidden * 4 // 7
    parts = ((0, cut), (cut, hidden))
    down_shard = down_weight.T
    gate_parts, up_parts, down_parts = [], [], []
    for start, stop in parts:
        gate_parts.append(gather_rows(gate_weight[:, start:stop]))
        up_parts.append(gather_rows(up_weight[:, start:stop]))
        down_parts.append(gather_rows(down_shard[:, start:stop]))

    j = jnp.arange(width)
    block, row = j // shard_rows, j % shard_rows
    far_c, far_m, at_o = block // (2 * outer), block // outer % 2, block % outer
    place = ((at_o * 2 + (far_m ^ my_m)) * 2 + (far_c ^ my_c)) * shard_rows + row
    order = (jnp.arange(width)[:, None] == place[None, :]).astype(bf16)
    token_low = jnp.dot(tokens, order, preferred_element_type=bf16)
    seed_all = jnp.dot(cotangent, order, preferred_element_type=bf16)
    gains = jnp.dot(jnp.stack([attn_gain, mlp_gain]), order, preferred_element_type=f32)
    attn_gain_f, mlp_gain_f = gains[0], gains[1]

    token_float = token_low.astype(f32)
    first_inverse = inverse_rms(token_float)
    first_rows = token_float * first_inverse
    first_normed = (first_rows * attn_gain_f).astype(bf16)
    cosine_table, sine_table = rotary_tables(seq_len, head_size)
    sine_table = jnp.where(jnp.arange(head_size) < head_size // 2, -sine_table, sine_table)
    attn_low, context_low, attn_part = attention(
        first_normed,
        attn_pieces,
        qkv_bias.astype(f32),
        cosine_table,
        sine_table,
        lengths,
        head_size,
    )
    attn_total = tensor_sum(attn_part)
    hidden_state = token_float + attn_total
    second_inverse = inverse_rms(hidden_state)
    second_rows = hidden_state * second_inverse
    second_normed = (second_rows * mlp_gain_f).astype(bf16)
    positions = jnp.arange(seq_len)
    valid_rows = (positions[None, :] < lengths[:, None]).reshape(token_rows, 1)
    seed_low = jnp.where(valid_rows, seed_all, jnp.zeros_like(seed_all))
    seed_grad = seed_low.astype(f32)
    gate_shares, up_shares, down_shares = [], [], []
    second_part = mlp_part = None
    for part, kind in enumerate((f32, bf16)):
        gate_value, up_value, activation = gate_up(second_normed, gate_parts[part], up_parts[part])
        down_shares.append(scatter_grad([seed_low], [activation], way=("zx", "xz")[part]))
        grad_gate, grad_up = gate_up_backward(seed_low, down_parts[part], gate_value, up_value)
        gate_shares.append(scatter_grad([second_normed], [grad_gate]))
        up_shares.append(scatter_grad([second_normed], [grad_up]))
        second_part = back_product(
            [grad_gate, grad_up], [gate_parts[part], up_parts[part]], second_part, kind
        )
        mlp_part = back_product([activation], [down_parts[part]], mlp_part, kind)
    second_grad = tensor_sum(second_part)
    mlp_total = tensor_sum(mlp_part)
    result = jnp.einsum(
        "tj,dj->td", (hidden_state + mlp_total).astype(bf16), order, preferred_element_type=bf16
    )
    grad_mlp_gain = jnp.sum(second_grad * second_rows, axis=0)
    hidden_grad = seed_grad + norm_backward(second_grad * mlp_gain_f, second_rows, second_inverse)
    hidden_low = hidden_grad.astype(bf16)
    out_share = scatter_grad([hidden_low], [context_low], way="direct")
    grad_mixed, first_part, grad_bias, grad_attn_gain = attention_backward(
        hidden_low, attn_low, attn_pieces, cosine_table, sine_table, lengths, first_rows, head_size
    )
    first_grad = tensor_sum(first_part)
    input_grad = hidden_grad + norm_backward(first_grad * attn_gain_f, first_rows, first_inverse)
    high = lax.reduce_precision(input_grad, 8, 7)
    rest = (input_grad - high).astype(bf16)
    grad_tokens = jnp.einsum(
        "tj,dj->td", high.astype(bf16), order, preferred_element_type=f32
    ) + jnp.einsum("tj,dj->td", rest, order, preferred_element_type=f32)

    grad_bias = grad_bias.reshape(outer, 2, 2, -1)
    bias_rows = grad_bias.shape[-1]
    grad_bias = jnp.where(my_c == 1, grad_bias[:, :, ::-1], grad_bias)
    grad_bias = jnp.where(my_m == 1, grad_bias[:, ::-1], grad_bias)
    grad_bias = jnp.pad(
        grad_bias.transpose(2, 1, 0, 3), ((0, 0), (0, 0), (0, 0), (0, shard_rows - bias_rows))
    ).reshape(width)
    vectors = jnp.stack([grad_attn_gain[0], grad_mlp_gain, grad_bias], axis=1)
    vectors = jnp.pad(vectors, ((0, 0), (0, 125)))
    qkv_share = scatter_grad([first_normed], [grad_mixed], vectors, "direct")
    vector_share = qkv_share[:, mixed_cols:]
    attn_gain_share = vector_share[:, 0]
    attn_gain_share = attn_gain_share + swap(attn_gain_share, "tensor")
    return (
        result,
        grad_tokens,
        qkv_share[:, None, :mixed_cols],
        vector_share[None, :bias_rows, 2],
        out_share.T[None],
        jnp.concatenate(gate_shares, axis=1),
        jnp.concatenate(up_shares, axis=1),
        jnp.concatenate(down_shares, axis=1).T,
        attn_gain_share,
        vector_share[:, 1],
    )


def solution(mesh):
    dp, tensor = mesh.shape["dp"], mesh.shape["tensor"]
    fine = Mesh(mesh.devices.reshape(dp // 4, 2, 2, tensor), ("o", "m", "c", "tensor"))
    data = ("o", "m", "c")
    return jax.shard_map(
        layer,
        mesh=fine,
        in_specs=(
            P(data, None),
            P(data),
            P(data, "tensor", None),
            P("tensor", None),
            P("tensor", None, data),
            P(data, "tensor"),
            P(data, "tensor"),
            P("tensor", data),
            P(),
            P(),
            P(data, None),
        ),
        out_specs=(
            P(data, None),
            P(data, None),
            P(data, "tensor", None),
            P("tensor", data),
            P("tensor", None, data),
            P(data, "tensor"),
            P(data, "tensor"),
            P("tensor", data),
            P(data),
            P(data),
        ),
        check_vma=False,
    )
```

```python
import jax
import jax.numpy as jnp
from jax import lax
from jax.experimental import pallas as pl
from jax.experimental.pallas import tpu as pltpu
from jax.sharding import Mesh
from jax.sharding import PartitionSpec as P


epsilon = 1e-06
SWAP = [(0, 1), (1, 0)]
bf16 = jnp.bfloat16
f32 = jnp.float32
Z, X, C, TENSOR = "z", "x", "c", "t"


def inverse_rms(values):
    return lax.rsqrt(jnp.mean(values * values, axis=-1, keepdims=True) + epsilon)


def norm_backward(grad_normed, normed_rows, inverse):
    return inverse * (
        grad_normed - normed_rows * jnp.mean(grad_normed * normed_rows, axis=-1, keepdims=True)
    )


def rotary_tables(length, head_size):
    half_size = head_size // 2
    frequency = jnp.power(10000.0, -jnp.arange(half_size, dtype=f32) * 2.0 / head_size)
    angles = jnp.arange(length, dtype=f32)[:, None] * frequency[None, :]
    angles = jnp.concatenate([angles, angles], axis=-1)
    return (jnp.cos(angles), jnp.sin(angles))


def swap(value, axis):
    return lax.ppermute(value, axis, SWAP)


def gather_rows(shard):
    own = lax.all_gather(shard, Z, axis=0, tiled=True)
    beside = swap(own, X)
    return (own, beside, swap(own, C), swap(beside, C))


def scatter_z(rows):
    return lax.psum_scatter(rows.astype(bf16), Z, scatter_dimension=0, tiled=True)


def scatter_z_direct(rows):
    outer = lax.axis_size(Z)
    me = lax.axis_index(Z)
    blocks = rows.reshape(outer, rows.shape[0] // outer, rows.shape[1])
    total = lax.dynamic_index_in_dim(blocks, me, 0, False)
    low = blocks.astype(bf16)
    for shift in range(1, outer):
        block = lax.dynamic_index_in_dim(low, lax.rem(me + shift, outer), 0, False)
        ring = [(i, (i + shift) % outer) for i in range(outer)]
        total = total + lax.ppermute(block, Z, ring).astype(f32)
    return total


def scatter_grad(lefts, rights, extra=None, z_first=False, direct=False):
    width = lefts[0].shape[1]
    half, quarter = width // 2, width // 4

    def rows(start, stop):
        pieces = [dot_tn(left[:, start:stop], right) for left, right in zip(lefts, rights)]
        if extra is not None:
            pieces.append(extra[start:stop])
        return pieces[0] if len(pieces) == 1 else jnp.concatenate(pieces, axis=1)

    came = swap(rows(half, width).astype(bf16), C)
    sent = rows(quarter, half) + came[quarter:].astype(f32)
    kept = rows(0, quarter) + came[:quarter].astype(f32)
    if z_first:
        beside = swap(scatter_z(sent), X)
        return scatter_z(kept).astype(f32) + beside.astype(f32)
    kept = kept + swap(sent.astype(bf16), X).astype(f32)
    return scatter_z_direct(kept) if direct else scatter_z(kept).astype(f32)


def tensor_sum(part):
    return part.astype(f32) + swap(part, TENSOR).astype(f32)


def dot(left, right):
    return jnp.dot(left, right, preferred_element_type=f32)


def dot_nt(left, right):
    return lax.dot_general(left, right, (((1,), (1,)), ((), ())), preferred_element_type=f32)


def dot_tn(left, right):
    return lax.dot_general(left, right, (((0,), (0,)), ((), ())), preferred_element_type=f32)


def tile_of(columns):
    return 512 if columns % 512 == 0 else 640


def whole(shape):
    return pl.BlockSpec(shape, lambda i: (0, 0))


def column_tile(rows, tile):
    return pl.BlockSpec((rows, tile), lambda i: (0, i))


def run(kernel, grid, in_specs, out_specs, out_shape, args, flops, scratch=()):
    moved = sum(a.size * a.dtype.itemsize for a in (*args, *out_shape))
    return pl.pallas_call(
        kernel,
        grid=(grid,),
        in_specs=in_specs,
        out_specs=out_specs,
        out_shape=out_shape,
        scratch_shapes=scratch,
        compiler_params=pltpu.CompilerParams(
            vmem_limit_bytes=56 << 20
        ),
        cost_estimate=pl.CostEstimate(flops=flops, bytes_accessed=moved, transcendentals=0),
    )(*args)


def stacked(refs):
    return jnp.concatenate([ref[...] for ref in refs], axis=0)


def gate_up(normed, gate, up):
    tokens, width = normed.shape
    columns = gate[0].shape[1]
    tile = tile_of(columns)

    def kernel(a_ref, *refs):
        gate_out, up_out, act_out = refs[8:]
        a = a_ref[...]
        g = dot(a, stacked(refs[:4]))
        u = dot(a, stacked(refs[4:8]))
        gate_out[...] = g
        up_out[...] = u
        act_out[...] = (g * jax.nn.sigmoid(g) * u).astype(bf16)

    out = column_tile(tokens, tile)
    return run(
        kernel,
        columns // tile,
        [whole((tokens, width))] + [column_tile(width // 4, tile)] * 8,
        [out] * 3,
        [jax.ShapeDtypeStruct((tokens, columns), t) for t in (f32, f32, bf16)],
        (normed, *gate, *up),
        4 * tokens * width * columns,
    )


def gate_up_backward(seed, down, gate, up):
    tokens, width = seed.shape
    columns = gate.shape[1]
    tile = tile_of(columns)

    def kernel(a_ref, d0, d1, d2, d3, gate_ref, up_ref, grad_gate, grad_up):
        grad = dot(a_ref[...], stacked((d0, d1, d2, d3)))
        g, u = gate_ref[...], up_ref[...]
        sigmoid = jax.nn.sigmoid(g)
        grad_gate[...] = (grad * u * sigmoid * (1.0 + g * (1.0 - sigmoid))).astype(bf16)
        grad_up[...] = (grad * (g * sigmoid)).astype(bf16)

    tiles = column_tile(tokens, tile)
    return run(
        kernel,
        columns // tile,
        [whole((tokens, width))] + [column_tile(width // 4, tile)] * 4 + [tiles] * 2,
        [tiles] * 2,
        [jax.ShapeDtypeStruct((tokens, columns), bf16)] * 2,
        (seed, *down, gate, up),
        2 * tokens * width * columns,
    )


def back_product(values, weights, before, out_type):
    tokens, columns = values[0].shape
    quarter = weights[0][0].shape[0]
    width = 4 * quarter
    tile = tile_of(columns)
    pairs = len(values)
    steps = columns // tile

    def kernel(*refs):
        value_refs, weight_refs = refs[:pairs], refs[pairs : 5 * pairs]
        out_ref, total = refs[-2:]
        step = pl.program_id(0)

        @pl.when(step == 0)
        def _():
            total[...] = jnp.zeros_like(total) if before is None else refs[5 * pairs][...]

        for piece in range(4):
            part = None
            for pair in range(pairs):
                term = dot_nt(value_refs[pair][...], weight_refs[4 * pair + piece][...])
                part = term if part is None else part + term
            total[:, piece * quarter : (piece + 1) * quarter] += part

        @pl.when(step == steps - 1)
        def _():
            out_ref[...] = total[...].astype(out_type)

    args = (*values, *(piece for weight in weights for piece in weight))
    specs = [column_tile(tokens, tile)] * pairs + [column_tile(quarter, tile)] * (4 * pairs)
    if before is not None:
        args, specs = args + (before,), specs + [whole((tokens, width))]
    return run(
        kernel,
        steps,
        specs,
        [whole((tokens, width))],
        [jax.ShapeDtypeStruct((tokens, width), out_type)],
        args,
        2 * pairs * tokens * width * columns,
        [pltpu.VMEM((tokens, width), f32)],
    )[0]


def visible_keys(length, size):
    query = lax.broadcasted_iota(jnp.int32, (size, size), 0)
    key = lax.broadcasted_iota(jnp.int32, (size, size), 1)
    return (key <= query) & (key < length)


def softmax_of(query, key, visible, scale):
    scores = jnp.where(visible, dot_nt(query, key) * scale, -jnp.inf)
    powers = jnp.exp(scores - jnp.max(scores, axis=-1, keepdims=True))
    return powers / jnp.sum(powers, axis=-1, keepdims=True)


def attention(normed, pieces, bias, cosine, sine, lengths, head):
    tokens, width = normed.shape
    seqs, size = lengths.shape[0], tokens // lengths.shape[0]
    quarter, mixed_cols = width // 4, bias.shape[1]
    group_cols = mixed_cols - 2 * head

    def kernel(len_ref, a_ref, p0, p1, p2, p3, bias_ref, cos_ref, sin_ref, low, context, out):
        weights = (p0, p1, p2, p3)
        weight = jnp.concatenate([ref[:, :mixed_cols] for ref in weights], axis=0)
        mixed = dot(a_ref[...], weight) + bias_ref[...]
        cos, sin = cos_ref[...], sin_ref[...]

        def rope(value):
            return (value * cos + pltpu.roll(value, head // 2, 1) * sin).astype(bf16)

        key = rope(mixed[:, group_cols : group_cols + head])
        value = mixed[:, group_cols + head :].astype(bf16)
        low[:, group_cols : group_cols + head] = key
        low[:, group_cols + head :] = value
        visible = visible_keys(len_ref[pl.program_id(0)], size)
        for start in range(0, group_cols, head):
            query = rope(mixed[:, start : start + head])
            low[:, start : start + head] = query
            probs = softmax_of(query, key, visible, head**-0.5).astype(bf16)
            context[:, start : start + head] = dot(probs, value).astype(bf16)
        for piece in range(4):
            out[:, piece * quarter : (piece + 1) * quarter] = dot_nt(
                context[...], weights[piece][:, mixed_cols:]
            ).astype(bf16)

    def rows(columns):
        return pl.BlockSpec((size, columns), lambda i: (i, 0))

    return run(
        kernel,
        seqs,
        [pl.BlockSpec(memory_space=pltpu.SMEM), rows(width)]
        + [whole(pieces[0].shape)] * 4
        + [whole(bias.shape), whole(cosine.shape), whole(sine.shape)],
        [rows(mixed_cols), rows(group_cols), rows(width)],
        [jax.ShapeDtypeStruct((tokens, c), bf16) for c in (mixed_cols, group_cols, width)],
        (lengths, normed, *pieces, bias, cosine, sine),
        2 * tokens * width * (mixed_cols + group_cols),
    )


def attention_backward(hidden_low, low, pieces, cosine, sine, lengths, normal, head):
    tokens, width = hidden_low.shape
    seqs, size = lengths.shape[0], tokens // lengths.shape[0]
    quarter, mixed_cols = width // 4, low.shape[1]
    group_cols = mixed_cols - 2 * head
    scale = head**-0.5

    def kernel(
        len_ref, h_ref, low_ref, p0, p1, p2, p3, cos_ref, sin_ref, normal_ref, mixed, part, bias, gain
    ):
        weights = (p0, p1, p2, p3)
        cos, sin = cos_ref[...], sin_ref[...]

        @pl.when(pl.program_id(0) == 0)
        def _():
            bias[...] = jnp.zeros_like(bias)
            gain[...] = jnp.zeros_like(gain)

        def keep(start, value, turn):
            if turn:
                value = value * cos - pltpu.roll(value, head // 2, 1) * sin
            rounded = value.astype(bf16)
            mixed[:, start : start + head] = rounded
            bias[:, start : start + head] += jnp.sum(
                rounded.astype(f32), axis=0, keepdims=True
            )

        out_weight = jnp.concatenate([ref[:, mixed_cols:] for ref in weights], axis=0)
        grad_context = dot(h_ref[...], out_weight).astype(bf16)
        key = low_ref[:, group_cols : group_cols + head]
        value = low_ref[:, group_cols + head :]
        visible = visible_keys(len_ref[pl.program_id(0)], size)
        grad_key = jnp.zeros((size, head), f32)
        grad_value = jnp.zeros((size, head), f32)
        for start in range(0, group_cols, head):
            query = low_ref[:, start : start + head]
            grad = grad_context[:, start : start + head]
            probs = softmax_of(query, key, visible, scale)
            grad_value += dot_tn(probs.astype(bf16), grad)
            grad_probs = dot_nt(grad, value)
            inner = jnp.sum(grad_probs * probs, axis=-1, keepdims=True)
            grad_scores = (probs * (grad_probs - inner)).astype(bf16)
            grad_key += dot_tn(grad_scores, query)
            keep(start, dot(grad_scores, key) * scale, True)
        keep(group_cols, grad_key * scale, True)
        keep(group_cols + head, grad_value, False)
        for piece in range(4):
            columns = slice(piece * quarter, (piece + 1) * quarter)
            term = dot_nt(mixed[...], weights[piece][:, :mixed_cols])
            part[:, columns] = term.astype(bf16)
            gain[:, columns] += jnp.sum(term * normal_ref[:, columns], axis=0, keepdims=True)

    def rows(columns):
        return pl.BlockSpec((size, columns), lambda i: (i, 0))

    return run(
        kernel,
        seqs,
        [pl.BlockSpec(memory_space=pltpu.SMEM), rows(width), rows(mixed_cols)]
        + [whole(pieces[0].shape)] * 4
        + [whole(cosine.shape), whole(sine.shape), rows(width)],
        [rows(mixed_cols), rows(width), whole((1, mixed_cols)), whole((1, width))],
        [
            jax.ShapeDtypeStruct((tokens, mixed_cols), bf16),
            jax.ShapeDtypeStruct((tokens, width), bf16),
            jax.ShapeDtypeStruct((1, mixed_cols), f32),
            jax.ShapeDtypeStruct((1, width), f32),
        ],
        (lengths, hidden_low, low, *pieces, cosine, sine, normal),
        2 * tokens * width * (mixed_cols + group_cols),
    )


def layer(
    tokens,
    lengths,
    qkv_weight,
    qkv_bias,
    out_weight,
    gate_weight,
    up_weight,
    down_weight,
    attn_gain,
    mlp_gain,
    cotangent,
):
    token_rows, width = tokens.shape
    seqs_here = lengths.shape[0]
    seq_len = token_rows // seqs_here
    group_cols = out_weight.shape[1]
    mixed_cols = qkv_weight.shape[2]
    head_size = (mixed_cols - group_cols) // 2
    shard_rows = qkv_weight.shape[0]
    outer = width // shard_rows // 4
    my_m, my_c = lax.axis_index(X), lax.axis_index(C)

    attn_shard = jnp.concatenate([qkv_weight[:, 0, :], out_weight[0].T], axis=1)
    attn_pieces = gather_rows(attn_shard)
    hidden = gate_weight.shape[1]
    cut = hidden * 4 // 7
    parts = ((0, cut), (cut, hidden))
    down_shard = down_weight.T
    gate_parts, up_parts, down_parts = [], [], []
    for start, stop in parts:
        gate_parts.append(gather_rows(gate_weight[:, start:stop]))
        up_parts.append(gather_rows(up_weight[:, start:stop]))
        down_parts.append(gather_rows(down_shard[:, start:stop]))

    j = jnp.arange(width)
    block, row = j // shard_rows, j % shard_rows
    far_c, far_m, at_o = block // (2 * outer), block // outer % 2, block % outer
    place = ((at_o * 2 + (far_m ^ my_m)) * 2 + (far_c ^ my_c)) * shard_rows + row
    order = (jnp.arange(width)[:, None] == place[None, :]).astype(bf16)
    token_low = jnp.dot(tokens, order, preferred_element_type=bf16)
    seed_all = jnp.dot(cotangent, order, preferred_element_type=bf16)
    gains = dot(jnp.stack([attn_gain, mlp_gain]), order)
    attn_gain_f, mlp_gain_f = gains[0], gains[1]
    valid_rows = (jnp.arange(seq_len)[None, :] < lengths[:, None]).reshape(token_rows, 1)
    seed_low = jnp.where(valid_rows, seed_all, jnp.zeros_like(seed_all))
    token_low, seed_low = lax.optimization_barrier((token_low, seed_low))
    seed_grad = seed_low.astype(f32)

    token_float = token_low.astype(f32)
    first_inverse = inverse_rms(token_float)
    first_rows = token_float * first_inverse
    first_normed = (first_rows * attn_gain_f).astype(bf16)
    cosine_table, sine_table = rotary_tables(seq_len, head_size)
    sine_table = jnp.where(jnp.arange(head_size) < head_size // 2, -sine_table, sine_table)
    attn_low, context_low, attn_part = attention(
        first_normed,
        attn_pieces,
        qkv_bias.astype(f32),
        cosine_table,
        sine_table,
        lengths,
        head_size,
    )
    attn_total = tensor_sum(attn_part)
    hidden_state = token_float + attn_total
    second_inverse = inverse_rms(hidden_state)
    second_rows = hidden_state * second_inverse
    second_normed = (second_rows * mlp_gain_f).astype(bf16)
    gate_shares, up_shares, down_shares = [], [], []
    second_part = mlp_part = None
    for part, kind in enumerate((f32, bf16)):
        gate_value, up_value, activation = gate_up(second_normed, gate_parts[part], up_parts[part])
        down_shares.append(scatter_grad([seed_low], [activation], z_first=part == 0))
        grad_gate, grad_up = gate_up_backward(seed_low, down_parts[part], gate_value, up_value)
        gate_shares.append(scatter_grad([second_normed], [grad_gate]))
        up_shares.append(scatter_grad([second_normed], [grad_up]))
        second_part = back_product(
            [grad_gate, grad_up], [gate_parts[part], up_parts[part]], second_part, kind
        )
        mlp_part = back_product([activation], [down_parts[part]], mlp_part, kind)
    second_grad = tensor_sum(second_part)
    mlp_total = tensor_sum(mlp_part)
    result = dot_nt((hidden_state + mlp_total).astype(bf16), order).astype(bf16)
    grad_mlp_gain = jnp.sum(second_grad * second_rows, axis=0)
    hidden_grad = seed_grad + norm_backward(second_grad * mlp_gain_f, second_rows, second_inverse)
    hidden_low = hidden_grad.astype(bf16)
    out_share = scatter_grad([hidden_low], [context_low], direct=True)
    grad_mixed, first_part, grad_bias, grad_attn_gain = attention_backward(
        hidden_low, attn_low, attn_pieces, cosine_table, sine_table, lengths, first_rows, head_size
    )
    first_grad = tensor_sum(first_part)
    input_grad = hidden_grad + norm_backward(first_grad * attn_gain_f, first_rows, first_inverse)
    high = lax.reduce_precision(input_grad, 8, 7)
    rest = (input_grad - high).astype(bf16)
    grad_tokens = dot_nt(high.astype(bf16), order) + dot_nt(rest, order)

    grad_bias = grad_bias.reshape(outer, 2, 2, -1)
    bias_rows = grad_bias.shape[-1]
    grad_bias = jnp.where(my_c == 1, grad_bias[:, :, ::-1], grad_bias)
    grad_bias = jnp.where(my_m == 1, grad_bias[:, ::-1], grad_bias)
    grad_bias = jnp.pad(
        grad_bias.transpose(2, 1, 0, 3), ((0, 0), (0, 0), (0, 0), (0, shard_rows - bias_rows))
    ).reshape(width)
    vectors = jnp.stack([grad_attn_gain[0], grad_mlp_gain, grad_bias], axis=1)
    vectors = jnp.pad(vectors, ((0, 0), (0, 125)))
    qkv_share = scatter_grad([first_normed], [grad_mixed], vectors, direct=True)
    vector_share = qkv_share[:, mixed_cols:]
    attn_gain_share = vector_share[:, 0]
    attn_gain_share = attn_gain_share + swap(attn_gain_share, TENSOR)
    return (
        result,
        grad_tokens,
        qkv_share[:, None, :mixed_cols],
        vector_share[None, :bias_rows, 2],
        out_share.T[None],
        jnp.concatenate(gate_shares, axis=1),
        jnp.concatenate(up_shares, axis=1),
        jnp.concatenate(down_shares, axis=1).T,
        attn_gain_share,
        vector_share[:, 1],
    )


def solution(mesh):
    dp, tensor = mesh.axis_names
    tensors = mesh.shape[tensor]
    fine = Mesh(
        mesh.devices.reshape(mesh.shape[dp] // 4, 2, 2, tensors), (Z, X, C, TENSOR)
    )
    data = (Z, X, C)
    weights = (P(data, TENSOR, None), P(TENSOR, None, data))
    hidden = (P(data, TENSOR), P(data, TENSOR), P(TENSOR, data))
    return jax.shard_map(
        layer,
        mesh=fine,
        in_specs=(
            P(data, None), P(data), weights[0], P(TENSOR, None), weights[1], *hidden,
            P(), P(), P(data, None),
        ),
        out_specs=(
            P(data, None), P(data, None), weights[0], P(TENSOR, data), weights[1], *hidden,
            P(data), P(data),
        ),
        check_vma=False,
    )
```

```python
import jax
import jax.numpy as jnp
from jax import lax
from jax.experimental import pallas as pl
from jax.experimental.pallas import tpu as pltpu
from jax.sharding import Mesh
from jax.sharding import PartitionSpec as P


epsilon = 1e-06
SWAP = [(0, 1), (1, 0)]
bf16 = jnp.bfloat16
f32 = jnp.float32
Z, X, C, TENSOR = "z", "x", "c", "t"


def inverse_rms(values):
    return lax.rsqrt(jnp.mean(values * values, axis=-1, keepdims=True) + epsilon)


def norm_backward(grad_normed, normed_rows, inverse):
    return inverse * (
        grad_normed - normed_rows * jnp.mean(grad_normed * normed_rows, axis=-1, keepdims=True)
    )


def rotary_tables(length, head_size):
    half_size = head_size // 2
    frequency = jnp.power(10000.0, -jnp.arange(half_size, dtype=f32) * 2.0 / head_size)
    angles = jnp.arange(length, dtype=f32)[:, None] * frequency[None, :]
    angles = jnp.concatenate([angles, angles], axis=-1)
    return (jnp.cos(angles), jnp.sin(angles))


def swap(value, axis):
    return lax.ppermute(value, axis, SWAP)


def gather_rows(shard):
    own = lax.all_gather(shard, Z, axis=0, tiled=True)
    beside = swap(own, X)
    return (own, beside, swap(own, C), swap(beside, C))


def scatter_z(rows):
    return lax.psum_scatter(rows.astype(bf16), Z, scatter_dimension=0, tiled=True)


def scatter_z_direct(rows):
    outer = lax.axis_size(Z)
    me = lax.axis_index(Z)
    blocks = rows.reshape(outer, rows.shape[0] // outer, rows.shape[1])
    total = lax.dynamic_index_in_dim(blocks, me, 0, False)
    low = blocks.astype(bf16)
    for shift in range(1, outer):
        block = lax.dynamic_index_in_dim(low, lax.rem(me + shift, outer), 0, False)
        ring = [(i, (i + shift) % outer) for i in range(outer)]
        total = total + lax.ppermute(block, Z, ring).astype(f32)
    return total


def scatter_grad(lefts, rights, extra=None, z_first=False, direct=False):
    width = lefts[0].shape[1]
    half, quarter = width // 2, width // 4

    def rows(start, stop):
        pieces = [dot_tn(left[:, start:stop], right) for left, right in zip(lefts, rights)]
        if extra is not None:
            pieces.append(extra[start:stop])
        return pieces[0] if len(pieces) == 1 else jnp.concatenate(pieces, axis=1)

    came = swap(rows(half, width).astype(bf16), C)
    if z_first:
        near = (rows(0, half) + came.astype(f32)).astype(bf16)
        near = lax.psum_scatter(near.reshape(2, quarter, -1), Z, scatter_dimension=1, tiled=True)
        return near[0].astype(f32) + swap(near[1], X).astype(f32)
    sent = rows(quarter, half) + came[quarter:].astype(f32)
    kept = rows(0, quarter) + came[:quarter].astype(f32)
    kept = kept + swap(sent.astype(bf16), X).astype(f32)
    return scatter_z_direct(kept) if direct else scatter_z(kept).astype(f32)


def tensor_sum(part):
    return part.astype(f32) + swap(part, TENSOR).astype(f32)


def dot(left, right):
    return jnp.dot(left, right, preferred_element_type=f32)


def dot_nt(left, right):
    return lax.dot_general(left, right, (((1,), (1,)), ((), ())), preferred_element_type=f32)


def dot_tn(left, right):
    return lax.dot_general(left, right, (((0,), (0,)), ((), ())), preferred_element_type=f32)


def tile_of(columns):
    return 512 if columns % 512 == 0 else 640


def whole(shape):
    return pl.BlockSpec(shape, lambda i: (0, 0))


def column_tile(rows, tile):
    return pl.BlockSpec((rows, tile), lambda i: (0, i))


def run(kernel, grid, in_specs, out_specs, out_shape, args, flops, scratch=()):
    moved = sum(a.size * a.dtype.itemsize for a in (*args, *out_shape))
    return pl.pallas_call(
        kernel,
        grid=(grid,),
        in_specs=in_specs,
        out_specs=out_specs,
        out_shape=out_shape,
        scratch_shapes=scratch,
        compiler_params=pltpu.CompilerParams(
            vmem_limit_bytes=56 << 20
        ),
        cost_estimate=pl.CostEstimate(flops=flops, bytes_accessed=moved, transcendentals=0),
    )(*args)


def stacked(refs):
    return jnp.concatenate([ref[...] for ref in refs], axis=0)


def gate_up(normed, gate, up):
    tokens, width = normed.shape
    columns = gate[0].shape[1]
    tile = tile_of(columns)

    def kernel(a_ref, *refs):
        gate_out, up_out, act_out = refs[8:]
        a = a_ref[...]
        g = dot(a, stacked(refs[:4]))
        u = dot(a, stacked(refs[4:8]))
        gate_out[...] = g
        up_out[...] = u
        act_out[...] = (g * jax.nn.sigmoid(g) * u).astype(bf16)

    out = column_tile(tokens, tile)
    return run(
        kernel,
        columns // tile,
        [whole((tokens, width))] + [column_tile(width // 4, tile)] * 8,
        [out] * 3,
        [jax.ShapeDtypeStruct((tokens, columns), t) for t in (f32, f32, bf16)],
        (normed, *gate, *up),
        4 * tokens * width * columns,
    )


def gate_up_backward(seed, down, gate, up):
    tokens, width = seed.shape
    columns = gate.shape[1]
    tile = tile_of(columns)

    def kernel(a_ref, d0, d1, d2, d3, gate_ref, up_ref, grad_gate, grad_up):
        grad = dot(a_ref[...], stacked((d0, d1, d2, d3)))
        g, u = gate_ref[...], up_ref[...]
        sigmoid = jax.nn.sigmoid(g)
        grad_gate[...] = (grad * u * sigmoid * (1.0 + g * (1.0 - sigmoid))).astype(bf16)
        grad_up[...] = (grad * (g * sigmoid)).astype(bf16)

    tiles = column_tile(tokens, tile)
    return run(
        kernel,
        columns // tile,
        [whole((tokens, width))] + [column_tile(width // 4, tile)] * 4 + [tiles] * 2,
        [tiles] * 2,
        [jax.ShapeDtypeStruct((tokens, columns), bf16)] * 2,
        (seed, *down, gate, up),
        2 * tokens * width * columns,
    )


def back_product(values, weights, before, out_type):
    tokens, columns = values[0].shape
    quarter = weights[0][0].shape[0]
    width = 4 * quarter
    tile = tile_of(columns)
    pairs = len(values)
    steps = columns // tile

    def kernel(*refs):
        value_refs, weight_refs = refs[:pairs], refs[pairs : 5 * pairs]
        out_ref, total = refs[-2:]
        step = pl.program_id(0)

        @pl.when(step == 0)
        def _():
            total[...] = jnp.zeros_like(total) if before is None else refs[5 * pairs][...]

        for piece in range(4):
            part = None
            for pair in range(pairs):
                term = dot_nt(value_refs[pair][...], weight_refs[4 * pair + piece][...])
                part = term if part is None else part + term
            total[:, piece * quarter : (piece + 1) * quarter] += part

        @pl.when(step == steps - 1)
        def _():
            out_ref[...] = total[...].astype(out_type)

    args = (*values, *(piece for weight in weights for piece in weight))
    specs = [column_tile(tokens, tile)] * pairs + [column_tile(quarter, tile)] * (4 * pairs)
    if before is not None:
        args, specs = args + (before,), specs + [whole((tokens, width))]
    return run(
        kernel,
        steps,
        specs,
        [whole((tokens, width))],
        [jax.ShapeDtypeStruct((tokens, width), out_type)],
        args,
        2 * pairs * tokens * width * columns,
        [pltpu.VMEM((tokens, width), f32)],
    )[0]


def visible_keys(length, size):
    query = lax.broadcasted_iota(jnp.int32, (size, size), 0)
    key = lax.broadcasted_iota(jnp.int32, (size, size), 1)
    return (key <= query) & (key < length)


def softmax_of(query, key, visible, scale):
    scores = jnp.where(visible, dot_nt(query, key) * scale, -jnp.inf)
    powers = jnp.exp(scores - jnp.max(scores, axis=-1, keepdims=True))
    return powers / jnp.sum(powers, axis=-1, keepdims=True)


def attention(normed, pieces, bias, cosine, sine, lengths, head):
    tokens, width = normed.shape
    seqs, size = lengths.shape[0], tokens // lengths.shape[0]
    quarter, mixed_cols = width // 4, bias.shape[1]
    group_cols = mixed_cols - 2 * head

    def kernel(len_ref, a_ref, p0, p1, p2, p3, bias_ref, cos_ref, sin_ref, low, context, out):
        weights = (p0, p1, p2, p3)
        weight = jnp.concatenate([ref[:, :mixed_cols] for ref in weights], axis=0)
        mixed = dot(a_ref[...], weight) + bias_ref[...]
        cos, sin = cos_ref[...], sin_ref[...]

        def rope(value):
            return (value * cos + pltpu.roll(value, head // 2, 1) * sin).astype(bf16)

        key = rope(mixed[:, group_cols : group_cols + head])
        value = mixed[:, group_cols + head :].astype(bf16)
        low[:, group_cols : group_cols + head] = key
        low[:, group_cols + head :] = value
        visible = visible_keys(len_ref[pl.program_id(0)], size)
        for start in range(0, group_cols, head):
            query = rope(mixed[:, start : start + head])
            low[:, start : start + head] = query
            probs = softmax_of(query, key, visible, head**-0.5).astype(bf16)
            context[:, start : start + head] = dot(probs, value).astype(bf16)
        for piece in range(4):
            out[:, piece * quarter : (piece + 1) * quarter] = dot_nt(
                context[...], weights[piece][:, mixed_cols:]
            ).astype(bf16)

    def rows(columns):
        return pl.BlockSpec((size, columns), lambda i: (i, 0))

    return run(
        kernel,
        seqs,
        [pl.BlockSpec(memory_space=pltpu.SMEM), rows(width)]
        + [whole(pieces[0].shape)] * 4
        + [whole(bias.shape), whole(cosine.shape), whole(sine.shape)],
        [rows(mixed_cols), rows(group_cols), rows(width)],
        [jax.ShapeDtypeStruct((tokens, c), bf16) for c in (mixed_cols, group_cols, width)],
        (lengths, normed, *pieces, bias, cosine, sine),
        2 * tokens * width * (mixed_cols + group_cols),
    )


def attention_backward(hidden_low, low, pieces, cosine, sine, lengths, normal, head):
    tokens, width = hidden_low.shape
    seqs, size = lengths.shape[0], tokens // lengths.shape[0]
    quarter, mixed_cols = width // 4, low.shape[1]
    group_cols = mixed_cols - 2 * head
    scale = head**-0.5

    def kernel(
        len_ref, h_ref, low_ref, p0, p1, p2, p3, cos_ref, sin_ref, normal_ref, mixed, part, bias, gain
    ):
        weights = (p0, p1, p2, p3)
        cos, sin = cos_ref[...], sin_ref[...]

        @pl.when(pl.program_id(0) == 0)
        def _():
            bias[...] = jnp.zeros_like(bias)
            gain[...] = jnp.zeros_like(gain)

        def keep(start, value, turn):
            if turn:
                value = value * cos - pltpu.roll(value, head // 2, 1) * sin
            rounded = value.astype(bf16)
            mixed[:, start : start + head] = rounded
            bias[:, start : start + head] += jnp.sum(
                rounded.astype(f32), axis=0, keepdims=True
            )

        out_weight = jnp.concatenate([ref[:, mixed_cols:] for ref in weights], axis=0)
        grad_context = dot(h_ref[...], out_weight).astype(bf16)
        key = low_ref[:, group_cols : group_cols + head]
        value = low_ref[:, group_cols + head :]
        visible = visible_keys(len_ref[pl.program_id(0)], size)
        grad_key = jnp.zeros((size, head), f32)
        grad_value = jnp.zeros((size, head), f32)
        for start in range(0, group_cols, head):
            query = low_ref[:, start : start + head]
            grad = grad_context[:, start : start + head]
            probs = softmax_of(query, key, visible, scale)
            grad_value += dot_tn(probs.astype(bf16), grad)
            grad_probs = dot_nt(grad, value)
            inner = jnp.sum(grad_probs * probs, axis=-1, keepdims=True)
            grad_scores = (probs * (grad_probs - inner)).astype(bf16)
            grad_key += dot_tn(grad_scores, query)
            keep(start, dot(grad_scores, key) * scale, True)
        keep(group_cols, grad_key * scale, True)
        keep(group_cols + head, grad_value, False)
        for piece in range(4):
            columns = slice(piece * quarter, (piece + 1) * quarter)
            term = dot_nt(mixed[...], weights[piece][:, :mixed_cols])
            part[:, columns] = term.astype(bf16)
            gain[:, columns] += jnp.sum(term * normal_ref[:, columns], axis=0, keepdims=True)

    def rows(columns):
        return pl.BlockSpec((size, columns), lambda i: (i, 0))

    return run(
        kernel,
        seqs,
        [pl.BlockSpec(memory_space=pltpu.SMEM), rows(width), rows(mixed_cols)]
        + [whole(pieces[0].shape)] * 4
        + [whole(cosine.shape), whole(sine.shape), rows(width)],
        [rows(mixed_cols), rows(width), whole((1, mixed_cols)), whole((1, width))],
        [
            jax.ShapeDtypeStruct((tokens, mixed_cols), bf16),
            jax.ShapeDtypeStruct((tokens, width), bf16),
            jax.ShapeDtypeStruct((1, mixed_cols), f32),
            jax.ShapeDtypeStruct((1, width), f32),
        ],
        (lengths, hidden_low, low, *pieces, cosine, sine, normal),
        2 * tokens * width * (mixed_cols + group_cols),
    )


def layer(
    tokens,
    lengths,
    qkv_weight,
    qkv_bias,
    out_weight,
    gate_weight,
    up_weight,
    down_weight,
    attn_gain,
    mlp_gain,
    cotangent,
):
    token_rows, width = tokens.shape
    seqs_here = lengths.shape[0]
    seq_len = token_rows // seqs_here
    group_cols = out_weight.shape[1]
    mixed_cols = qkv_weight.shape[2]
    head_size = (mixed_cols - group_cols) // 2
    shard_rows = qkv_weight.shape[0]
    outer = width // shard_rows // 4
    my_m, my_c = lax.axis_index(X), lax.axis_index(C)

    attn_shard = jnp.concatenate([qkv_weight[:, 0, :], out_weight[0].T], axis=1)
    attn_pieces = gather_rows(attn_shard)
    hidden = gate_weight.shape[1]
    cut = hidden * 4 // 7
    parts = ((0, cut), (cut, hidden))
    down_shard = down_weight.T
    gate_parts, up_parts, down_parts = [], [], []
    for start, stop in parts:
        gate_parts.append(gather_rows(gate_weight[:, start:stop]))
        up_parts.append(gather_rows(up_weight[:, start:stop]))
        down_parts.append(gather_rows(down_shard[:, start:stop]))

    j = jnp.arange(width)
    block, row = j // shard_rows, j % shard_rows
    far_c, far_m, at_o = block // (2 * outer), block // outer % 2, block % outer
    place = ((at_o * 2 + (far_m ^ my_m)) * 2 + (far_c ^ my_c)) * shard_rows + row
    order = (jnp.arange(width)[:, None] == place[None, :]).astype(bf16)
    token_low = jnp.dot(tokens, order, preferred_element_type=bf16)
    seed_all = jnp.dot(cotangent, order, preferred_element_type=bf16)
    gains = dot(jnp.stack([attn_gain, mlp_gain]), order)
    attn_gain_f, mlp_gain_f = gains[0], gains[1]
    valid_rows = (jnp.arange(seq_len)[None, :] < lengths[:, None]).reshape(token_rows, 1)
    seed_low = jnp.where(valid_rows, seed_all, jnp.zeros_like(seed_all))
    token_low, seed_low = lax.optimization_barrier((token_low, seed_low))
    seed_grad = seed_low.astype(f32)

    token_float = token_low.astype(f32)
    first_inverse = inverse_rms(token_float)
    first_rows = token_float * first_inverse
    first_normed = (first_rows * attn_gain_f).astype(bf16)
    cosine_table, sine_table = rotary_tables(seq_len, head_size)
    sine_table = jnp.where(jnp.arange(head_size) < head_size // 2, -sine_table, sine_table)
    attn_low, context_low, attn_part = attention(
        first_normed,
        attn_pieces,
        qkv_bias.astype(f32),
        cosine_table,
        sine_table,
        lengths,
        head_size,
    )
    attn_total = tensor_sum(attn_part)
    hidden_state = token_float + attn_total
    second_inverse = inverse_rms(hidden_state)
    second_rows = hidden_state * second_inverse
    second_normed = (second_rows * mlp_gain_f).astype(bf16)
    gate_shares, up_shares, down_shares = [], [], []
    second_part = mlp_part = None
    for part, kind in enumerate((f32, bf16)):
        gate_value, up_value, activation = gate_up(second_normed, gate_parts[part], up_parts[part])
        down_shares.append(scatter_grad([seed_low], [activation], z_first=part == 0))
        grad_gate, grad_up = gate_up_backward(seed_low, down_parts[part], gate_value, up_value)
        gate_shares.append(scatter_grad([second_normed], [grad_gate]))
        up_shares.append(scatter_grad([second_normed], [grad_up]))
        second_part = back_product(
            [grad_gate, grad_up], [gate_parts[part], up_parts[part]], second_part, kind
        )
        mlp_part = back_product([activation], [down_parts[part]], mlp_part, kind)
    second_grad = tensor_sum(second_part)
    mlp_total = tensor_sum(mlp_part)
    result = dot_nt((hidden_state + mlp_total).astype(bf16), order).astype(bf16)
    grad_mlp_gain = jnp.sum(second_grad * second_rows, axis=0)
    hidden_grad = seed_grad + norm_backward(second_grad * mlp_gain_f, second_rows, second_inverse)
    hidden_low = hidden_grad.astype(bf16)
    out_share = scatter_grad([hidden_low], [context_low], direct=True)
    grad_mixed, first_part, grad_bias, grad_attn_gain = attention_backward(
        hidden_low, attn_low, attn_pieces, cosine_table, sine_table, lengths, first_rows, head_size
    )
    first_grad = tensor_sum(first_part)
    input_grad = hidden_grad + norm_backward(first_grad * attn_gain_f, first_rows, first_inverse)
    high = lax.reduce_precision(input_grad, 8, 7)
    rest = (input_grad - high).astype(bf16)
    grad_tokens = dot_nt(high.astype(bf16), order) + dot_nt(rest, order)

    grad_bias = grad_bias.reshape(outer, 2, 2, -1)
    bias_rows = grad_bias.shape[-1]
    grad_bias = jnp.where(my_c == 1, grad_bias[:, :, ::-1], grad_bias)
    grad_bias = jnp.where(my_m == 1, grad_bias[:, ::-1], grad_bias)
    grad_bias = jnp.pad(
        grad_bias.transpose(2, 1, 0, 3), ((0, 0), (0, 0), (0, 0), (0, shard_rows - bias_rows))
    ).reshape(width)
    vectors = jnp.stack([grad_attn_gain[0], grad_mlp_gain, grad_bias], axis=1)
    vectors = jnp.pad(vectors, ((0, 0), (0, 125)))
    qkv_share = scatter_grad([first_normed], [grad_mixed], vectors, direct=True)
    vector_share = qkv_share[:, mixed_cols:]
    attn_gain_share = vector_share[:, 0]
    attn_gain_share = attn_gain_share + swap(attn_gain_share, TENSOR)
    return (
        result,
        grad_tokens,
        qkv_share[:, None, :mixed_cols],
        vector_share[None, :bias_rows, 2],
        out_share.T[None],
        jnp.concatenate(gate_shares, axis=1),
        jnp.concatenate(up_shares, axis=1),
        jnp.concatenate(down_shares, axis=1).T,
        attn_gain_share,
        vector_share[:, 1],
    )


def solution(mesh):
    dp, tensor = mesh.axis_names
    tensors = mesh.shape[tensor]
    fine = Mesh(
        mesh.devices.reshape(mesh.shape[dp] // 4, 2, 2, tensors), (Z, X, C, TENSOR)
    )
    data = (Z, X, C)
    weights = (P(data, TENSOR, None), P(TENSOR, None, data))
    hidden = (P(data, TENSOR), P(data, TENSOR), P(TENSOR, data))
    return jax.shard_map(
        layer,
        mesh=fine,
        in_specs=(
            P(data, None), P(data), weights[0], P(TENSOR, None), weights[1], *hidden,
            P(), P(), P(data, None),
        ),
        out_specs=(
            P(data, None), P(data, None), weights[0], P(TENSOR, data), weights[1], *hidden,
            P(data), P(data),
        ),
        check_vma=False,
    )
```
